256 devices in a mesh: island: 8 (over x, z_hi), own: 32 (over z_lo, y, core).
Axes of the slice: x: 4, y: 4, z: 8 (z_hi: 2, z_lo: 4; z = z_hi * 4 + z_lo), core: 2. Of those that a mesh axis runs over, the one named last changes fastest.
Arguments:
- master: float32 [8, 2048, 8192], P(None, ('island', 'own')), may hold values from -6 to 6
- momentum: float32 [8, 2048, 8192], P(None, ('island', 'own')), may hold values from -6 to 6
- deltas: float32 [8, 2048, 8192], P('island', None, 'own'), may hold values from -6 to 6
- old_path: int32 [8], replicated, may hold values from 0 to 255
- new_path: int32 [8], replicated, may hold values from 0 to 255
- path_module: int32 [256], replicated, may hold values from 0 to 7
- island_steps: int32 [8], replicated, may hold values from 1 to 9
Outputs:
- new_master: float32 [8, 2048, 8192], P(None, ('island', 'own'))
- new_momentum: float32 [8, 2048, 8192], P(None, ('island', 'own'))
- new_module: float32 [8, 2048, 8192], P('island', None, 'own')
The draws below stay inside these ranges and needn't reach their ends.
All inputs are finite; a program needn't handle non-finite values.
Results may differ from the reference program's by a relative error of at most 0.00007.
Values sent between devices are 32-bit elements; how exact they have to be, the bound alone decides.
No kernel may reach another device: no remote copies, remote signals or barrier semaphores. Data moves between devices by JAX's collectives and lax.ppermute only.
A program may use at most 64 MiB of HBM per device.

```python
import jax
import jax.numpy as jnp
from jax import lax

R = 2048
C = 8192
MODULES = 8
PATHS = 256
ISL = 8


def place_ends(result, rng, smallest, high):
    place = [jax.random.randint(jax.random.fold_in(rng, axis), (), 0, length) for axis, length in enumerate(result.shape)]
    widest = result.shape.index(max(result.shape))
    beside = place[:widest] + [(place[widest] + 1) % result.shape[widest]] + place[widest + 1:]
    return result.at[tuple(place)].set(smallest).at[tuple(beside)].set(high)


def block_scale(key, extent, pieces, smallest, largest):
    factor_of, own = 1.0, jax.random.fold_in(key, 6)
    for axis_at, shards_of in pieces:
        heights = jnp.exp(jax.random.uniform(jax.random.fold_in(own, axis_at), (shards_of,), jnp.float32, smallest / len(pieces), largest / len(pieces)))
        factor_of = factor_of * jnp.repeat(heights, extent[axis_at] // shards_of).reshape([-1 if axis == axis_at else 1 for axis in range(len(extent))])
    return factor_of


def bell_draw(stream_key, shape, width, bound, shards=(), kind=jnp.bfloat16):
    result = jax.random.normal(stream_key, shape, jnp.float32) * width
    if len(shards) > 0:
        result = block_scale(stream_key, shape, shards, -0.22, 0.18) * result
    return jnp.clip(result, min=-bound, max=bound).astype(kind)


def setup_inputs(seed: int = 0) -> dict:
    keys = jax.random.split(jax.random.key(seed), 8)
    master = bell_draw(keys[0], (MODULES, R, C), 1.0, 6.0, ((1, 256),), jnp.float32)
    momentum = bell_draw(keys[1], (MODULES, R, C), 1.0, 6.0, ((1, 256),), jnp.float32)
    deltas = bell_draw(keys[2], (ISL, R, C), 1.0, 6.0, ((0, 8), (2, 32)), jnp.float32)
    old_path = place_ends(jax.random.randint(keys[3], (ISL,), 0, PATHS), jax.random.fold_in(keys[3], 1), 0, PATHS - 1).astype(jnp.int32)
    new_path = place_ends(jax.random.randint(keys[4], (ISL,), 0, PATHS), jax.random.fold_in(keys[4], 1), 0, PATHS - 1).astype(jnp.int32)
    path_module = place_ends(jax.random.randint(keys[5], (PATHS,), 0, MODULES), jax.random.fold_in(keys[5], 1), 0, MODULES - 1).astype(jnp.int32)
    island_steps = place_ends(jax.random.randint(keys[6], (ISL,), 1, 10), jax.random.fold_in(keys[6], 1), 1, 9).astype(jnp.int32)
    return {"master": master, "momentum": momentum, "deltas": deltas, "old_path": old_path, "new_path": new_path, "path_module": path_module, "island_steps": island_steps}


def reference(master, momentum, deltas, old_path, new_path, path_module, island_steps):
    old_module = path_module[old_path].astype(jnp.int32)
    chosen = old_module[None, :] == jnp.arange(MODULES, dtype=jnp.int32)[:, None]
    mixing = chosen.astype(jnp.float32) * island_steps.astype(jnp.float32)[None, :]
    divisor = jnp.maximum(jnp.sum(mixing, axis=1), 1.0)
    average = jnp.einsum("kj,jrc->krc", mixing, deltas, precision=lax.Precision.HIGHEST)
    average = average / divisor[:, None, None]
    new_momentum = 0.9 * momentum + average
    new_master = master - 0.7 * (average + 0.9 * new_momentum)
    new_index = path_module[new_path].astype(jnp.int32)
    new_module = jnp.take(new_master, new_index, axis=0)
    return new_master, new_momentum, new_module
```

```python
import math

import jax
import jax.numpy as jnp
from jax import lax
from jax.experimental import pallas as pl
from jax.experimental.pallas import tpu as pltpu
from jax.sharding import Mesh
from jax.sharding import PartitionSpec as P

Z = ("zh", "zl")
PLANE = ("x", "y", "c")
NX, NZ, NYC = 4, 8, 8
NP = NX * NYC
SHIFTS = (4, 3, 5, 2, 6, 1, 7)
TILE = (8, 128)
F32 = jnp.float32
MIB = 1 << 20


def tiles(value):
    lead, rows, cols = value.shape[:-2], value.shape[-2], value.shape[-1]
    value = value.reshape(*lead, rows // 8, 8, cols // 128, 128)
    return jnp.swapaxes(value, -3, -2)


def call(body, ins, outs, scalars=1, limit=16 * MIB, **kw):
    smem = pl.BlockSpec(memory_space=pltpu.SMEM)
    vmem = pl.BlockSpec(memory_space=pltpu.VMEM)
    moved = 4 * (sum(a.size for a in ins[scalars:]) + sum(math.prod(s) for s in outs))
    return pl.pallas_call(
        body,
        out_shape=[jax.ShapeDtypeStruct(s, F32) for s in outs],
        in_specs=[smem] * scalars + [vmem] * (len(ins) - scalars),
        out_specs=[vmem] * len(outs),
        cost_estimate=pl.CostEstimate(flops=moved, bytes_accessed=moved, transcendentals=0),
        compiler_params=pltpu.CompilerParams(vmem_limit_bytes=limit),
        **kw,
    )(*ins)


def part(x):
    return pl.ds(x * NYC, NYC)


def cut_kernel(z_ref, d_ref, *outs):
    z = z_ref[0]
    for d in range(NZ):
        to = lax.rem(z + d, NZ)
        for x in range(NX):
            rows = pl.ds(x * NZ * NYC + to * NYC, NYC)
            outs[d][part(x)] = d_ref[rows, 0]
            outs[NZ][part(x), d] = d_ref[rows, 1]


def stack_kernel(*refs):
    for d in range(NZ):
        refs[NZ][:, d] = refs[d][...]


def unstack_kernel(src, *outs):
    for d in range(NZ):
        outs[d][...] = src[:, d]


def weights(modules, old_ref, pm_ref, steps_ref, k):
    mix = []
    total = jnp.int32(0)
    for j in range(steps_ref.shape[0]):
        w = jnp.where(pm_ref[old_ref[j]] == k, steps_ref[j], 0)
        total += w
        mix.append(w)
    inverse = 1.0 / jnp.full(TILE, jnp.maximum(total, 1), jnp.int32).astype(F32)
    return [w.astype(F32) for w in mix], inverse


def average(read, mix, inverse, d, same):
    total = None
    for x in range(NX):
        for e in range(2):
            lo, hi = mix[2 * x], mix[2 * x + 1]
            w = jnp.where(same == e, lo, hi)
            term = w * read(x, d + 4 * e)
            total = term if total is None else total + term
    return total * inverse


def held_by(z, d):
    other = lax.rem(z - d + NZ, NZ)
    return other >> 2, other & 3


def step(m, v, avg):
    v = 0.9 * v + avg
    return m - 0.7 * (avg + 0.9 * v), v


def pick_kernel(half, split, z_ref, old_ref, new_ref, pm_ref, steps_ref, *refs):
    z = z_ref[0]
    n = NZ if split else 1
    src, (m_ref, v_ref), outs = refs[:n], refs[n : n + 2], refs[n + 2 :]
    read = lambda x, d: src[d][part(x)] if split else src[0][part(x), d]
    for j in range(steps_ref.shape[0]):
        k = pm_ref[new_ref[j]]
        mix, inverse = weights(m_ref.shape[0], old_ref, pm_ref, steps_ref, k)
        for d in range(4):
            same, place = held_by(z, d)
            avg = average(read, mix, inverse, d, same)
            new, _ = step(m_ref[k, place, :, half], v_ref[k, place, :, half], avg)
            near, far = (NZ - d) % NZ, (NZ + 4 - d) % NZ
            here = j % 2 == same
            if split:
                for way, pick in ((near, here), (far, jnp.logical_not(here))):

                    @pl.when(pick)
                    def _():
                        outs[way][part(j // 2)] = new
            else:
                outs[0][part(j // 2), jnp.where(here, near, far)] = new


def owner_kernel(z_ref, old_ref, pm_ref, steps_ref, *refs):
    z = z_ref[0]
    a_ref, b_refs, (m_ref, v_ref, nm_ref, nv_ref) = refs[0], refs[1 : 1 + NZ], refs[1 + NZ :]
    reads = (lambda x, d: a_ref[part(x), d], lambda x, d: b_refs[d][part(x)])
    for k in range(m_ref.shape[0]):
        mix, inverse = weights(m_ref.shape[0], old_ref, pm_ref, steps_ref, k)
        for d in range(4):
            same, place = held_by(z, d)
            for half in range(2):
                avg = average(reads[half], mix, inverse, d, same)
                new, mom = step(m_ref[k, place, :, half], v_ref[k, place, :, half], avg)
                nm_ref[k, place, :, half] = new
                nv_ref[k, place, :, half] = mom


def join_kernel(z_ref, b_ref, *refs):
    z = z_ref[0]
    for d in range(NZ):
        source = lax.rem(z - d + NZ, NZ)
        for x in range(NX):
            rows = pl.ds(x * NZ * NYC + source * NYC, NYC)
            refs[NZ][rows, 0] = refs[d][part(x)]
            refs[NZ][rows, 1] = b_ref[part(x), d]


def along_z(pieces):
    got = [pieces[0]] + [None] * (NZ - 1)
    for d in SHIFTS:
        got[d] = lax.ppermute(pieces[d], Z, [(i, (i + d) % NZ) for i in range(NZ)])
    return got


def in_plane(value):
    return lax.all_to_all(value, PLANE, split_axis=0, concat_axis=0, tiled=True)


def shards(master, momentum, deltas, old_path, new_path, path_module, island_steps):
    modules = master.shape[0]
    z = lax.axis_index(Z).astype(jnp.int32).reshape(1)
    piece, packed = (NP, *TILE), (NP, NZ, *TILE)
    owner = (modules, 4, NYC, 2, *TILE)
    m = tiles(master).reshape(owner)
    v = tiles(momentum).reshape(owner)
    d = tiles(deltas[0])

    *a, b = call(cut_kernel, [z, d], [piece] * NZ + [packed])
    a = along_z(a)
    b = in_plane(b)
    [a] = call(stack_kernel, a, [packed], scalars=0)
    b = call(unstack_kernel, [b], [piece] * NZ, scalars=0)
    b = along_z(b)
    a = in_plane(a)

    def pick(half, split, *src):
        body = lambda *refs: pick_kernel(half, split, *refs)
        outs = [piece] * NZ if split else [packed]
        return call(body, [z, old_path, new_path, path_module, island_steps, *src, m, v], outs, scalars=5)

    [pa] = pick(0, False, a)
    pb = pick(1, True, *b)
    nm, nv = call(owner_kernel, [z, old_path, path_module, island_steps, a, *b, m, v], [owner] * 2, scalars=4, limit=24 * MIB)
    pa = in_plane(pa)
    pb = along_z(pb)
    pa = call(unstack_kernel, [pa], [piece] * NZ, scalars=0)
    [pb] = call(stack_kernel, pb, [packed], scalars=0)
    pa = along_z(pa)
    pb = in_plane(pb)
    [out] = call(join_kernel, [z, pb, *pa], [d.shape])

    def whole(value):
        return jnp.swapaxes(value.reshape(modules, 64, *TILE), 1, 2).reshape(master.shape)

    new_module = jnp.swapaxes(out, 1, 2).reshape(deltas.shape)
    return whole(nm), whole(nv), new_module


def solution(mesh):
    fine = Mesh(mesh.devices.reshape(4, 2, 4, 4, 2), ("x", "zh", "zl", "y", "c"))
    owners = P(None, ("x", "zh", "zl", "y", "c"), None)
    island = P(("x", "zh"), None, ("zl", "y", "c"))
    return jax.shard_map(
        shards,
        mesh=fine,
        in_specs=(owners, owners, island, P(), P(), P(), P()),
        out_specs=(owners, owners, island),
        check_vma=False,
    )
```

```python
import math

import jax
import jax.numpy as jnp
from jax import lax
from jax.experimental import pallas as pl
from jax.experimental.pallas import tpu as pltpu
from jax.sharding import Mesh
from jax.sharding import PartitionSpec as P

XZ = ("x", "zh", "zl")
YC = ("y", "c")
NY, NC = 4, 2
NYC = NY * NC
SHIFTS = (4, 5, 2, 6, 3, 7, 1)
TILE = (8, 128)
F32 = jnp.float32
MIB = 1 << 20


def tiles(value):
    lead, rows, cols = value.shape[:-2], value.shape[-2], value.shape[-1]
    value = value.reshape(*lead, rows // 8, 8, cols // 128, 128)
    return jnp.swapaxes(value, -3, -2)


def call(body, ins, outs, scalars, limit=16 * MIB):
    smem = pl.BlockSpec(memory_space=pltpu.SMEM)
    vmem = pl.BlockSpec(memory_space=pltpu.VMEM)
    moved = 4 * (sum(a.size for a in ins[scalars:]) + sum(math.prod(s) for s in outs))
    return pl.pallas_call(
        body,
        out_shape=[jax.ShapeDtypeStruct(s, F32) for s in outs],
        in_specs=[smem] * scalars + [vmem] * (len(ins) - scalars),
        out_specs=[vmem] * len(outs),
        cost_estimate=pl.CostEstimate(flops=moved, bytes_accessed=moved, transcendentals=0),
        compiler_params=pltpu.CompilerParams(vmem_limit_bytes=limit),
    )(*ins)


def ahead(me, d):
    return ((((me >> 1) + d // NC) & (NY - 1)) << 1) | ((me & 1) ^ (d % NC))


def behind(me, d):
    return ((((me >> 1) + NY - d // NC) & (NY - 1)) << 1) | ((me & 1) ^ (d % NC))


def base_kernel(me_ref, m_ref, v_ref, *outs):
    for d in range(NYC):
        at = ahead(me_ref[0], d)
        outs[d][...] = m_ref[:, :, at] - (0.7 * 0.81) * v_ref[:, :, at]


def mix_kernel(me_ref, old_ref, new_ref, pm_ref, steps_ref, r_ref, *refs):
    me = me_ref[0]
    bases, averages, out = refs[:NYC], refs[NYC : 2 * NYC], refs[2 * NYC]
    islands = steps_ref.shape[0]
    old = [pm_ref[old_ref[j]] for j in range(islands)]
    new = [pm_ref[new_ref[j]] for j in range(islands)]
    weights = []
    for j in range(islands):
        total = jnp.int32(0)
        for i in range(islands):
            total += jnp.where(old[i] == old[j], steps_ref[i], 0)
        splat = lambda s: jnp.full(TILE, s, jnp.int32).astype(F32)
        weights.append(splat(steps_ref[j]) / splat(jnp.maximum(total, 1)))
    for d in range(NYC):
        rows = ahead(me, d)
        e = ((NY - d // NC) % NY) * NC + d % NC
        averages[d][...] = jnp.zeros(averages[d].shape, F32)
        for j in range(islands):
            averages[d][old[j]] += weights[j] * r_ref[j, :, rows]
        for j in range(islands):
            out[j, :, rows] = bases[e][new[j]] - (0.7 * 1.9) * averages[d][new[j]]


def owner_kernel(me_ref, m_ref, v_ref, *refs):
    averages, (nm_ref, nv_ref) = refs[:NYC], refs[NYC:]
    for d in range(NYC):
        at = behind(me_ref[0], d)
        avg = averages[d][...]
        mom = 0.9 * v_ref[:, :, at] + avg
        nv_ref[:, :, at] = mom
        nm_ref[:, :, at] = m_ref[:, :, at] - 0.7 * (avg + 0.9 * mom)


def along_yc(pieces):
    got = [pieces[0]] + [None] * (NYC - 1)
    for d in SHIFTS:
        got[d] = lax.ppermute(pieces[d], YC, [(i, ahead(i, d)) for i in range(NYC)])
    return got


def across_xz(value):
    return lax.all_to_all(value, XZ, split_axis=0, concat_axis=0, tiled=True)


def shards(master, momentum, deltas, old_path, new_path, path_module, island_steps):
    modules = master.shape[0]
    me = lax.axis_index(YC).astype(jnp.int32).reshape(1)
    owner = (modules, 4, NYC, 2, *TILE)
    piece = (modules, 4, 2, *TILE)
    m = tiles(master).reshape(owner)
    v = tiles(momentum).reshape(owner)

    got = across_xz(deltas[0].reshape(32, 64, 256))
    base = along_yc(call(base_kernel, [me, m, v], [piece] * NYC, 1))
    isles = (8, 4, NYC, 2, *TILE)
    *avg, out = call(
        mix_kernel,
        [me, old_path, new_path, path_module, island_steps, tiles(got).reshape(isles), *base],
        [piece] * NYC + [isles],
        5,
    )
    out = jnp.swapaxes(out.reshape(32, NYC, 2, *TILE), 2, 3).reshape(32, 64, 256)
    new_module = across_xz(out).reshape(deltas.shape)
    nm, nv = call(owner_kernel, [me, m, v, *along_yc(avg)], [owner] * 2, 1)

    def whole(value):
        return jnp.swapaxes(value.reshape(modules, 64, *TILE), 1, 2).reshape(master.shape)

    return whole(nm), whole(nv), new_module


def solution(mesh):
    fine = Mesh(mesh.devices.reshape(4, 2, 4, 4, 2), ("x", "zh", "zl", "y", "c"))
    owners = P(None, ("x", "zh", "zl", "y", "c"), None)
    island = P(("x", "zh"), None, ("zl", "y", "c"))
    return jax.shard_map(
        shards,
        mesh=fine,
        in_specs=(owners, owners, island, P(), P(), P(), P()),
        out_specs=(owners, owners, island),
        check_vma=False,
    )
```

```python
import math

import jax
import jax.numpy as jnp
from jax import lax
from jax.experimental import pallas as pl
from jax.experimental.pallas import tpu as pltpu
from jax.sharding import Mesh
from jax.sharding import PartitionSpec as P

XZ = ("x", "zh", "zl")
YC = ("y", "c")
NY, NC = 4, 2
NYC = NY * NC
SHIFTS = (4, 5, 2, 6, 3, 7, 1)
TILE = (8, 128)
F32 = jnp.float32
MIB = 1 << 20


def tiles(value):
    lead, rows, cols = value.shape[:-2], value.shape[-2], value.shape[-1]
    value = value.reshape(*lead, rows // 8, 8, cols // 128, 128)
    return jnp.swapaxes(value, -3, -2)


def call(body, ins, outs, scalars, scratch, sems, limit=64 * MIB - MIB // 4):
    smem = pl.BlockSpec(memory_space=pltpu.SMEM)
    hbm = pl.BlockSpec(memory_space=pltpu.HBM)
    moved = 4 * (sum(a.size for a in ins[scalars:]) + sum(math.prod(s) for s in outs))
    return pl.pallas_call(
        body,
        out_shape=[jax.ShapeDtypeStruct(s, F32) for s in outs],
        in_specs=[smem] * scalars + [hbm] * (len(ins) - scalars),
        out_specs=[hbm] * len(outs),
        scratch_shapes=[pltpu.VMEM(s, F32) for s in scratch] + [pltpu.SemaphoreType.DMA((sems, NYC))],
        cost_estimate=pl.CostEstimate(flops=moved, bytes_accessed=moved, transcendentals=0),
        compiler_params=pltpu.CompilerParams(vmem_limit_bytes=limit),
    )(*ins)


def started(copies):
    for copy in copies:
        copy.start()
    return copies


def ahead(me, d):
    return ((((me >> 1) + d // NC) & (NY - 1)) << 1) | ((me & 1) ^ (d % NC))


def behind(me, d):
    return ((((me >> 1) + NY - d // NC) & (NY - 1)) << 1) | ((me & 1) ^ (d % NC))


def base_kernel(me_ref, m_ref, v_ref, *refs):
    outs, (m_buf, v_buf, sem) = refs[:NYC], refs[NYC:]
    copy = pltpu.make_async_copy
    at = [ahead(me_ref[0], d) for d in range(NYC)]
    ms = [copy(m_ref.at[:, :, at[d]], m_buf.at[d], sem.at[0, d]) for d in range(NYC)]
    vs = [copy(v_ref.at[:, :, at[d]], v_buf.at[d], sem.at[1, d]) for d in range(NYC)]
    order = (*SHIFTS, 0)
    for d in order:
        started([ms[d], vs[d]])
    back = []
    for d in order:
        ms[d].wait()
        vs[d].wait()
        m_buf[d] -= (0.7 * 0.81) * v_buf[d]
        back += started([copy(m_buf.at[d], outs[d], sem.at[2, d])])
    for done in back:
        done.wait()


def mix_kernel(me_ref, old_ref, new_ref, pm_ref, steps_ref, r_ref, *refs):
    me = me_ref[0]
    bases, averages, out = refs[:NYC], refs[NYC : 2 * NYC], refs[2 * NYC]
    r_buf, b_buf, a_buf, o_buf, sem = refs[2 * NYC + 1 :]
    copy = pltpu.make_async_copy
    rows = [ahead(me, d) for d in range(NYC)]
    opposite = [((NY - d // NC) % NY) * NC + d % NC for d in range(NYC)]
    rs = [copy(r_ref.at[:, :, rows[d]], r_buf.at[d], sem.at[0, d]) for d in range(NYC)]
    bs = [copy(bases[opposite[d]], b_buf.at[d], sem.at[1, d]) for d in range(NYC)]
    for d in range(NYC):
        started([rs[d], bs[d]])
    islands = steps_ref.shape[0]
    old = [pm_ref[old_ref[j]] for j in range(islands)]
    new = [pm_ref[new_ref[j]] for j in range(islands)]
    weights = []
    for j in range(islands):
        total = jnp.int32(0)
        for i in range(islands):
            total += jnp.where(old[i] == old[j], steps_ref[i], 0)
        splat = lambda s: jnp.full(TILE, s, jnp.int32).astype(F32)
        weights.append(splat(steps_ref[j]) / splat(jnp.maximum(total, 1)))
    back = []
    for d in range(NYC):
        a_buf[d] = jnp.zeros(a_buf.shape[1:], F32)
        rs[d].wait()
        for j in range(islands):
            a_buf[d, old[j]] += weights[j] * r_buf[d, j]
        bs[d].wait()
        for j in range(islands):
            o_buf[d, j] = b_buf[d, new[j]] - (0.7 * 1.9) * a_buf[d, new[j]]
        back += started(
            [
                copy(o_buf.at[d], out.at[:, :, rows[d]], sem.at[2, d]),
                copy(a_buf.at[d], averages[d], sem.at[3, d]),
            ]
        )
    for done in back:
        done.wait()


def owner_kernel(me_ref, m_ref, v_ref, *refs):
    averages, (nm_ref, nv_ref), (m_buf, v_buf, a_buf, sem) = refs[:NYC], refs[NYC : NYC + 2], refs[NYC + 2 :]
    copy = pltpu.make_async_copy
    at = [behind(me_ref[0], d) for d in range(NYC)]
    ins = []
    for d in range(NYC):
        ins.append(
            started(
                [
                    copy(m_ref.at[:, :, at[d]], m_buf.at[d], sem.at[0, d]),
                    copy(v_ref.at[:, :, at[d]], v_buf.at[d], sem.at[1, d]),
                    copy(averages[d], a_buf.at[d], sem.at[2, d]),
                ]
            )
        )
    back = []
    for d in range(NYC):
        for done in ins[d]:
            done.wait()
        avg = a_buf[d]
        mom = 0.9 * v_buf[d] + avg
        v_buf[d] = mom
        m_buf[d] -= 0.7 * (avg + 0.9 * mom)
        back += started(
            [
                copy(m_buf.at[d], nm_ref.at[:, :, at[d]], sem.at[3, d]),
                copy(v_buf.at[d], nv_ref.at[:, :, at[d]], sem.at[4, d]),
            ]
        )
    for done in back:
        done.wait()


def place_kernel(src, out, sem):
    step = src.shape[0] // NYC
    for done in started(
        [
            pltpu.make_async_copy(src.at[pl.ds(d * step, step)], out.at[pl.ds(d * step, step)], sem.at[0, d])
            for d in range(NYC)
        ]
    ):
        done.wait()


def along_yc(pieces):
    got = [pieces[0]] + [None] * (NYC - 1)
    for d in SHIFTS:
        got[d] = lax.ppermute(pieces[d], YC, [(i, ahead(i, d)) for i in range(NYC)])
    return got


def across_xz(value):
    return lax.all_to_all(value, XZ, split_axis=0, concat_axis=0, tiled=True)


def shards(master, momentum, deltas, old_path, new_path, path_module, island_steps):
    modules = master.shape[0]
    me = lax.axis_index(YC).astype(jnp.int32).reshape(1)
    owner = (modules, 4, NYC, 2, *TILE)
    piece = (modules, 4, 2, *TILE)
    m = tiles(master).reshape(owner)
    v = tiles(momentum).reshape(owner)

    got = across_xz(deltas[0].reshape(32, 64, 256))
    slots = (NYC, *piece)
    base = along_yc(call(base_kernel, [me, m, v], [piece] * NYC, 1, [slots] * 2, 3))
    isles = (8, 4, NYC, 2, *TILE)
    *avg, out = call(
        mix_kernel,
        [me, old_path, new_path, path_module, island_steps, tiles(got).reshape(isles), *base],
        [piece] * NYC + [isles],
        5,
        [slots] * 4,
        4,
    )
    out = jnp.swapaxes(out.reshape(32, NYC, 2, *TILE), 2, 3).reshape(32, 64, 256)
    landed = across_xz(out)
    nm, nv = call(owner_kernel, [me, m, v, *along_yc(avg)], [owner] * 2, 1, [slots] * 3, 5)
    [new_module] = call(place_kernel, [landed], [landed.shape], 0, [], 1)
    new_module = new_module.reshape(deltas.shape)

    def whole(value):
        return jnp.swapaxes(value.reshape(modules, 64, *TILE), 1, 2).reshape(master.shape)

    return whole(nm), whole(nv), new_module


def solution(mesh):
    fine = Mesh(mesh.devices.reshape(4, 2, 4, 4, 2), ("x", "zh", "zl", "y", "c"))
    owners = P(None, ("x", "zh", "zl", "y", "c"), None)
    island = P(("x", "zh"), None, ("zl", "y", "c"))
    return jax.shard_map(
        shards,
        mesh=fine,
        in_specs=(owners, owners, island, P(), P(), P(), P()),
        out_specs=(owners, owners, island),
        check_vma=False,
    )
```

```python
import math

import jax
import jax.numpy as jnp
from jax import lax
from jax.experimental import pallas as pl
from jax.experimental.pallas import tpu as pltpu
from jax.sharding import Mesh
from jax.sharding import PartitionSpec as P

XZ = ("x", "zh", "zl")
ZX = ("zh", "zl", "x")
YC = ("y", "c")
NY, NC, NZ = 4, 2, 8
NYC = NY * NC
SHIFTS = (4, 5, 2, 6, 3, 7, 1)
TILE = (8, 128)
F32 = jnp.float32
MIB = 1 << 20


def tiles(value):
    lead, rows, cols = value.shape[:-2], value.shape[-2], value.shape[-1]
    value = value.reshape(*lead, rows // 8, 8, cols // 128, 128)
    return jnp.swapaxes(value, -3, -2)


def call(body, ins, outs, scalars, scratch, sems, limit=64 * MIB - MIB // 4, near=()):
    smem = pl.BlockSpec(memory_space=pltpu.SMEM)
    hbm = pl.BlockSpec(memory_space=pltpu.HBM)
    vmem = pl.BlockSpec(memory_space=pltpu.VMEM)
    moved = 4 * (sum(a.size for a in ins[scalars:]) + sum(math.prod(s) for s in outs))
    return pl.pallas_call(
        body,
        out_shape=[jax.ShapeDtypeStruct(s, F32) for s in outs],
        in_specs=[smem] * scalars + [hbm] * (len(ins) - scalars),
        out_specs=[vmem if i in near else hbm for i in range(len(outs))],
        scratch_shapes=[pltpu.VMEM(s, F32) for s in scratch] + [pltpu.SemaphoreType.DMA((sems, NYC))],
        cost_estimate=pl.CostEstimate(flops=moved, bytes_accessed=moved, transcendentals=0),
        compiler_params=pltpu.CompilerParams(vmem_limit_bytes=limit),
    )(*ins)


def started(copies):
    for copy in copies:
        copy.start()
    return copies


def ahead(me, d):
    return ((((me >> 1) + d // NC) & (NY - 1)) << 1) | ((me & 1) ^ (d % NC))


def behind(me, d):
    return ((((me >> 1) + NY - d // NC) & (NY - 1)) << 1) | ((me & 1) ^ (d % NC))


def base_kernel(me_ref, m_ref, v_ref, *refs):
    outs, (m_buf, v_buf, sem) = refs[:NYC], refs[NYC:]
    copy = pltpu.make_async_copy
    at = [ahead(me_ref[0], d) for d in range(NYC)]
    ms = [copy(m_ref.at[:, :, at[d]], m_buf.at[d], sem.at[0, d]) for d in range(NYC)]
    vs = [copy(v_ref.at[:, :, at[d]], v_buf.at[d], sem.at[1, d]) for d in range(NYC)]
    order = (*SHIFTS, 0)
    for d in order:
        started([ms[d], vs[d]])
    back = []
    for d in order:
        ms[d].wait()
        vs[d].wait()
        m_buf[d] -= (0.7 * 0.81) * v_buf[d]
        back += started([copy(m_buf.at[d], outs[d], sem.at[2, d])])
    for done in back:
        done.wait()


def mix_kernel(me_ref, old_ref, new_ref, pm_ref, steps_ref, r_ref, *refs):
    me = me_ref[0]
    bases, averages, out = refs[:NYC], refs[NYC : 2 * NYC], refs[2 * NYC]
    r_buf, b_buf, a_buf, sem = refs[2 * NYC + 1 :]
    copy = pltpu.make_async_copy
    rows = [ahead(me, d) for d in range(NYC)]
    opposite = [((NY - d // NC) % NY) * NC + d % NC for d in range(NYC)]
    rs = [copy(r_ref.at[:, :, rows[d]], r_buf.at[d], sem.at[0, d]) for d in range(NYC)]
    bs = [copy(bases[opposite[d]], b_buf.at[d], sem.at[1, d]) for d in range(NYC)]
    for d in range(NYC):
        started([rs[d], bs[d]])
    islands = steps_ref.shape[0]
    old = [pm_ref[old_ref[j]] for j in range(islands)]
    new = [pm_ref[new_ref[j]] for j in range(islands)]
    weights = []
    for j in range(islands):
        total = jnp.int32(0)
        for i in range(islands):
            total += jnp.where(old[i] == old[j], steps_ref[i], 0)
        splat = lambda s: jnp.full(TILE, s, jnp.int32).astype(F32)
        weights.append(splat(steps_ref[j]) / splat(jnp.maximum(total, 1)))
    back = []
    for d in range(NYC):
        a_buf[d] = jnp.zeros(a_buf.shape[1:], F32)
        rs[d].wait()
        for j in range(islands):
            a_buf[d, old[j]] += weights[j] * r_buf[d, j]
        bs[d].wait()
        for j in range(islands):
            out[j % 2, :, j // 2, rows[d]] = b_buf[d, new[j]] - (0.7 * 1.9) * a_buf[d, new[j]]
        back += started([copy(a_buf.at[d], averages[d], sem.at[2, d])])
    for done in back:
        done.wait()


def owner_kernel(me_ref, m_ref, v_ref, *refs):
    averages, (nm_ref, nv_ref), (m_buf, v_buf, a_buf, sem) = refs[:NYC], refs[NYC : NYC + 2], refs[NYC + 2 :]
    copy = pltpu.make_async_copy
    at = [behind(me_ref[0], d) for d in range(NYC)]
    ins = []
    for d in range(NYC):
        ins.append(
            started(
                [
                    copy(m_ref.at[:, :, at[d]], m_buf.at[d], sem.at[0, d]),
                    copy(v_ref.at[:, :, at[d]], v_buf.at[d], sem.at[1, d]),
                    copy(averages[d], a_buf.at[d], sem.at[2, d]),
                ]
            )
        )
    back = []
    for d in range(NYC):
        for done in ins[d]:
            done.wait()
        avg = a_buf[d]
        mom = 0.9 * v_buf[d] + avg
        v_buf[d] = mom
        m_buf[d] -= 0.7 * (avg + 0.9 * mom)
        back += started(
            [
                copy(m_buf.at[d], nm_ref.at[:, :, at[d]], sem.at[3, d]),
                copy(v_buf.at[d], nv_ref.at[:, :, at[d]], sem.at[4, d]),
            ]
        )
    for done in back:
        done.wait()


def place_kernel(src, out, buf, sem):
    copy = pltpu.make_async_copy
    ins = started([copy(src.at[z], buf.at[:, z], sem.at[0, z]) for z in range(NZ)])
    back = []
    for z in range(NZ):
        ins[z].wait()
        back += started([copy(buf.at[:, z], out.at[:, z], sem.at[1, z])])
    for done in back:
        done.wait()


def along_yc(pieces):
    got = [pieces[0]] + [None] * (NYC - 1)
    for d in SHIFTS:
        got[d] = lax.ppermute(pieces[d], YC, [(i, ahead(i, d)) for i in range(NYC)])
    return got


def across(axes, value):
    return lax.all_to_all(value, axes, split_axis=0, concat_axis=0, tiled=True)


def shards(master, momentum, deltas, old_path, new_path, path_module, island_steps):
    modules = master.shape[0]
    me = lax.axis_index(YC).astype(jnp.int32).reshape(1)
    owner = (modules, 4, NYC, 2, *TILE)
    piece = (modules, 4, 2, *TILE)
    m = tiles(master).reshape(owner)
    v = tiles(momentum).reshape(owner)

    got = across(XZ, deltas[0].reshape(32, 64, 256))
    slots = (NYC, *piece)
    base = along_yc(call(base_kernel, [me, m, v], [piece] * NYC, 1, [slots] * 2, 3))
    isles, sent = (8, 4, NYC, 2, *TILE), (2, 4, 4, NYC, 2, *TILE)
    *avg, out = call(
        mix_kernel,
        [me, old_path, new_path, path_module, island_steps, tiles(got).reshape(isles), *base],
        [piece] * NYC + [sent],
        5,
        [slots] * 3,
        3,
        limit=64 * MIB - MIB // 4,
        near=(NYC,),
    )
    out = jnp.swapaxes(out.reshape(32, NYC, 2, *TILE), 2, 3).reshape(32, 64, 256)
    landed = across(ZX, out)
    nm, nv = call(owner_kernel, [me, m, v, *along_yc(avg)], [owner] * 2, 1, [slots] * 3, 5)
    landed = landed.reshape(NZ, 4, 64, 256)
    placed = (4, NZ, 64, 256)
    [new_module] = call(place_kernel, [landed], [placed], 0, [placed], 2)
    new_module = new_module.reshape(deltas.shape)

    def whole(value):
        return jnp.swapaxes(value.reshape(modules, 64, *TILE), 1, 2).reshape(master.shape)

    return whole(nm), whole(nv), new_module


def solution(mesh):
    fine = Mesh(mesh.devices.reshape(4, 2, 4, 4, 2), ("x", "zh", "zl", "y", "c"))
    owners = P(None, ("x", "zh", "zl", "y", "c"), None)
    island = P(("x", "zh"), None, ("zl", "y", "c"))
    return jax.shard_map(
        shards,
        mesh=fine,
        in_specs=(owners, owners, island, P(), P(), P(), P()),
        out_specs=(owners, owners, island),
        check_vma=False,
    )
```

```python
import math

import jax
import jax.numpy as jnp
from jax import lax
from jax.experimental import pallas as pl
from jax.experimental.pallas import tpu as pltpu
from jax.sharding import Mesh
from jax.sharding import PartitionSpec as P

XZ = ("x", "zh", "zl")
YC = ("y", "c")
NY, NC = 4, 2
NYC = NY * NC
SHIFTS = (4, 5, 2, 6, 3, 7, 1)
TILE = (8, 128)
F32 = jnp.float32
MIB = 1 << 20
WHOLE = 64 * MIB - MIB // 4


def tiles(value):
    lead, rows, cols = value.shape[:-2], value.shape[-2], value.shape[-1]
    value = value.reshape(*lead, rows // 8, 8, cols // 128, 128)
    return jnp.swapaxes(value, -3, -2)


def call(body, ins, outs, scalars, scratch, sems, limit):
    smem, hbm = (pl.BlockSpec(memory_space=m) for m in (pltpu.SMEM, pltpu.HBM))
    moved = 4 * (sum(a.size for a in ins[scalars:]) + sum(math.prod(s) for s in outs))
    return pl.pallas_call(
        body,
        out_shape=[jax.ShapeDtypeStruct(s, F32) for s in outs],
        in_specs=[smem] * scalars + [hbm] * (len(ins) - scalars),
        out_specs=[hbm] * len(outs),
        scratch_shapes=[pltpu.VMEM(s, F32) for s in scratch] + [pltpu.SemaphoreType.DMA((sems, NYC))],
        cost_estimate=pl.CostEstimate(flops=moved, bytes_accessed=moved, transcendentals=0),
        compiler_params=pltpu.CompilerParams(vmem_limit_bytes=limit),
    )(*ins)


def started(copies):
    for copy in copies:
        copy.start()
    return copies


def ahead(me, d):
    return ((((me >> 1) + d // NC) & (NY - 1)) << 1) | ((me & 1) ^ (d % NC))


def behind(me, d):
    return ((((me >> 1) + NY - d // NC) & (NY - 1)) << 1) | ((me & 1) ^ (d % NC))


def base_kernel(me_ref, m_ref, v_ref, *refs):
    outs, (m_buf, v_buf, sem) = refs[:NYC], refs[NYC:]
    copy = pltpu.make_async_copy
    at = [ahead(me_ref[0], d) for d in range(NYC)]
    ms = [copy(m_ref.at[:, :, at[d]], m_buf.at[d], sem.at[0, d]) for d in range(NYC)]
    vs = [copy(v_ref.at[:, :, at[d]], v_buf.at[d], sem.at[1, d]) for d in range(NYC)]
    order = (*SHIFTS, 0)
    for d in order:
        started([ms[d], vs[d]])
    back = []
    for d in order:
        ms[d].wait()
        vs[d].wait()
        m_buf[d] -= (0.7 * 0.81) * v_buf[d]
        back += started([copy(m_buf.at[d], outs[d], sem.at[2, d])])
    for done in back:
        done.wait()


def mix_kernel(me_ref, old_ref, new_ref, pm_ref, steps_ref, r_ref, *refs):
    me = me_ref[0]
    bases, averages, out = refs[:NYC], refs[NYC : 2 * NYC], refs[2 * NYC]
    r_buf, b_buf, o_buf, a_buf, sem = refs[2 * NYC + 1 :]
    copy = pltpu.make_async_copy
    rows = [ahead(me, d) for d in range(NYC)]
    opposite = [((NY - d // NC) % NY) * NC + d % NC for d in range(NYC)]
    rs = [copy(r_ref.at[:, :, rows[d]], r_buf.at[d], sem.at[0, d]) for d in range(NYC)]
    bs = [copy(bases[opposite[d]], b_buf.at[d], sem.at[3, d]) for d in range(NYC)]
    for d in range(NYC):
        started([rs[d], bs[d]])
    islands = steps_ref.shape[0]
    old = [pm_ref[old_ref[j]] for j in range(islands)]
    new = [pm_ref[new_ref[j]] for j in range(islands)]
    weights = []
    for j in range(islands):
        total = jnp.int32(0)
        for i in range(islands):
            total += jnp.where(old[i] == old[j], steps_ref[i], 0)
        splat = lambda s: jnp.full(TILE, s, jnp.int32).astype(F32)
        weights.append(splat(steps_ref[j]) / splat(jnp.maximum(total, 1)))
    back = []
    for d in range(NYC):
        avg = a_buf.at[d]
        avg[...] = jnp.zeros(avg.shape, F32)
        rs[d].wait()
        for j in range(islands):
            avg[old[j]] += weights[j] * r_buf[d, j]
        bs[d].wait()
        for j in range(islands):
            o_buf[d, j] = b_buf[d, new[j]] - (0.7 * 1.9) * avg[new[j]]
        back += started([copy(o_buf.at[d], out.at[:, :, rows[d]], sem.at[1, d])])
    for d in range(NYC):
        back += started([copy(a_buf.at[d], averages[d], sem.at[2, d])])
    for done in back:
        done.wait()


def owner_kernel(me_ref, m_ref, v_ref, *refs):
    averages, (nm_ref, nv_ref), (m_buf, v_buf, a_buf, sem) = refs[:NYC], refs[NYC : NYC + 2], refs[NYC + 2 :]
    copy = pltpu.make_async_copy
    at = [behind(me_ref[0], d) for d in range(NYC)]
    ins = []
    for d in range(NYC):
        ins.append(
            started(
                [
                    copy(m_ref.at[:, :, at[d]], m_buf.at[d], sem.at[0, d]),
                    copy(v_ref.at[:, :, at[d]], v_buf.at[d], sem.at[1, d]),
                    copy(averages[d], a_buf.at[d], sem.at[2, d]),
                ]
            )
        )
    back = []
    for d in range(NYC):
        for done in ins[d]:
            done.wait()
        avg = a_buf[d]
        mom = 0.9 * v_buf[d] + avg
        v_buf[d] = mom
        m_buf[d] -= 0.7 * (avg + 0.9 * mom)
        back += started(
            [
                copy(m_buf.at[d], nm_ref.at[:, :, at[d]], sem.at[3, d]),
                copy(v_buf.at[d], nv_ref.at[:, :, at[d]], sem.at[4, d]),
            ]
        )
    for done in back:
        done.wait()


def along_yc(pieces):
    got = [pieces[0]] + [None] * (NYC - 1)
    for d in SHIFTS:
        got[d] = lax.ppermute(pieces[d], YC, [(i, ahead(i, d)) for i in range(NYC)])
    return got


def across(value):
    return lax.all_to_all(value, XZ, split_axis=0, concat_axis=0, tiled=True)


def shards(master, momentum, deltas, old_path, new_path, path_module, island_steps):
    modules = master.shape[0]
    me = lax.axis_index(YC).astype(jnp.int32).reshape(1)
    owner = (modules, 4, NYC, 2, *TILE)
    piece = (modules, 4, 2, *TILE)
    m = tiles(master).reshape(owner)
    v = tiles(momentum).reshape(owner)

    got = across(deltas[0].reshape(32, 64, 256))
    slots = (NYC, *piece)
    base = along_yc(call(base_kernel, [me, m, v], [piece] * NYC, 1, [slots] * 2, 3, WHOLE))
    isles = (8, 4, NYC, 2, *TILE)
    *avg, out = call(
        mix_kernel,
        [me, old_path, new_path, path_module, island_steps, tiles(got).reshape(isles), *base],
        [piece] * NYC + [isles],
        5,
        [slots] * 4,
        4,
        WHOLE,
    )
    out = jnp.swapaxes(out.reshape(32, NYC, 2, *TILE), 2, 3).reshape(32, 64, 256)
    landed = across(out)
    nm, nv = call(owner_kernel, [me, m, v, *along_yc(avg)], [owner] * 2, 1, [slots] * 3, 5, 61 * MIB)
    new_module = landed.reshape(deltas.shape)

    def whole(value):
        return jnp.swapaxes(value.reshape(modules, 64, *TILE), 1, 2).reshape(master.shape)

    return whole(nm), whole(nv), new_module


def solution(mesh):
    fine = Mesh(mesh.devices.reshape(4, 2, 4, 4, 2), ("x", "zh", "zl", "y", "c"))
    owners = P(None, ("x", "zh", "zl", "y", "c"), None)
    island = P(("x", "zh"), None, ("zl", "y", "c"))
    return jax.shard_map(
        shards,
        mesh=fine,
        in_specs=(owners, owners, island, P(), P(), P(), P()),
        out_specs=(owners, owners, island),
        check_vma=False,
    )
```

```python
import math

import jax
import jax.numpy as jnp
from jax import lax
from jax.experimental import pallas as pl
from jax.experimental.pallas import tpu as pltpu
from jax.sharding import Mesh
from jax.sharding import PartitionSpec as P

XZ = ("x", "zh", "zl")
YC = ("y", "c")
NY, NC = 4, 2
NYC = NY * NC
SHIFTS = (4, 5, 2, 6, 3, 7, 1)
TILE = (8, 128)
F32 = jnp.float32
MIB = 1 << 20
WHOLE = 64 * MIB - MIB // 4


def tiles(value):
    lead, rows, cols = value.shape[:-2], value.shape[-2], value.shape[-1]
    value = value.reshape(*lead, rows // 8, 8, cols // 128, 128)
    return jnp.swapaxes(value, -3, -2)


def call(body, ins, outs, scalars, scratch, sems, limit, near_in=(), near_out=()):
    smem, vmem, hbm = (pl.BlockSpec(memory_space=m) for m in (pltpu.SMEM, pltpu.VMEM, pltpu.HBM))
    moved = 4 * (sum(a.size for a in ins[scalars:]) + sum(math.prod(s) for s in outs))
    return pl.pallas_call(
        body,
        out_shape=[jax.ShapeDtypeStruct(s, F32) for s in outs],
        in_specs=[smem] * scalars + [vmem if i in near_in else hbm for i in range(scalars, len(ins))],
        out_specs=[vmem if i in near_out else hbm for i in range(len(outs))],
        scratch_shapes=[pltpu.VMEM(s, F32) for s in scratch] + [pltpu.SemaphoreType.DMA((sems, NYC))],
        cost_estimate=pl.CostEstimate(flops=moved, bytes_accessed=moved, transcendentals=0),
        compiler_params=pltpu.CompilerParams(vmem_limit_bytes=limit),
    )(*ins)


def started(copies):
    for copy in copies:
        copy.start()
    return copies


def ahead(me, d):
    return ((((me >> 1) + d // NC) & (NY - 1)) << 1) | ((me & 1) ^ (d % NC))


def behind(me, d):
    return ((((me >> 1) + NY - d // NC) & (NY - 1)) << 1) | ((me & 1) ^ (d % NC))


def base_kernel(me_ref, m_ref, v_ref, *refs):
    outs, (m_buf, v_buf, sem) = refs[:NYC], refs[NYC:]
    copy = pltpu.make_async_copy
    at = [ahead(me_ref[0], d) for d in range(NYC)]
    ms = [copy(m_ref.at[:, :, at[d]], m_buf.at[d], sem.at[0, d]) for d in range(NYC)]
    vs = [copy(v_ref.at[:, :, at[d]], v_buf.at[d], sem.at[1, d]) for d in range(NYC)]
    order = (*SHIFTS, 0)
    for d in order:
        started([ms[d], vs[d]])
    back = []
    for d in order:
        ms[d].wait()
        vs[d].wait()
        m_buf[d] -= (0.7 * 0.81) * v_buf[d]
        back += started([copy(m_buf.at[d], outs[d], sem.at[2, d])])
    for done in back:
        done.wait()


def weigh(old_ref, pm_ref, steps_ref):
    islands = steps_ref.shape[0]
    old = [pm_ref[old_ref[j]] for j in range(islands)]
    weights = []
    for j in range(islands):
        total = jnp.int32(0)
        for i in range(islands):
            total += jnp.where(old[i] == old[j], steps_ref[i], 0)
        splat = lambda s: jnp.full(TILE, s, jnp.int32).astype(F32)
        weights.append(splat(steps_ref[j]) / splat(jnp.maximum(total, 1)))
    return list(zip(old, weights))


def add_up(avg, deltas, weighted):
    avg[...] = jnp.zeros(avg.shape, F32)
    for j, (k, w) in enumerate(weighted):
        avg[k] += w * deltas[j]


def hold_kernel(src, out, sem):
    out[...] = src[...]


def pick_kernel(me_ref, old_ref, new_ref, pm_ref, steps_ref, r_ref, *refs):
    me = me_ref[0]
    bases, (out, r_buf, o_buf, avg, sem) = refs[:NYC], refs[NYC:]
    copy = pltpu.make_async_copy
    rows = [behind(me, d) for d in range(NYC)]
    rs = started([copy(r_ref.at[:, :, rows[d]], r_buf.at[d], sem.at[0, d]) for d in range(NYC)])
    weighted = weigh(old_ref, pm_ref, steps_ref)
    back = []
    for d in range(NYC):
        rs[d].wait()
        add_up(avg, r_buf.at[d], weighted)
        for j in range(steps_ref.shape[0]):
            k = pm_ref[new_ref[j]]
            o_buf[d, j] = bases[d][k] - (0.7 * 1.9) * avg[k]
        back += started([copy(o_buf.at[d], out.at[:, :, rows[d]], sem.at[1, d])])
    for done in back:
        done.wait()


def average_kernel(me_ref, old_ref, pm_ref, steps_ref, r_ref, *refs):
    averages, (r_buf, a_buf, sem) = refs[:NYC], refs[NYC:]
    copy = pltpu.make_async_copy
    rows = [ahead(me_ref[0], d) for d in range(NYC)]
    order = (*SHIFTS, 0)
    rs = [copy(r_ref.at[:, :, rows[d]], r_buf.at[d], sem.at[0, d]) for d in range(NYC)]
    started([rs[d] for d in order])
    weighted = weigh(old_ref, pm_ref, steps_ref)
    back = []
    for d in order:
        rs[d].wait()
        add_up(a_buf.at[d], r_buf.at[d], weighted)
        back += started([copy(a_buf.at[d], averages[d], sem.at[1, d])])
    for done in back:
        done.wait()


def owner_kernel(me_ref, m_ref, v_ref, *refs):
    averages, (nm_ref, nv_ref), (m_buf, v_buf, a_buf, sem) = refs[:NYC], refs[NYC : NYC + 2], refs[NYC + 2 :]
    copy = pltpu.make_async_copy
    at = [behind(me_ref[0], d) for d in range(NYC)]
    ins = []
    for d in range(NYC):
        ins.append(
            started(
                [
                    copy(m_ref.at[:, :, at[d]], m_buf.at[d], sem.at[0, d]),
                    copy(v_ref.at[:, :, at[d]], v_buf.at[d], sem.at[1, d]),
                    copy(averages[d], a_buf.at[d], sem.at[2, d]),
                ]
            )
        )
    back = []
    for d in range(NYC):
        for done in ins[d]:
            done.wait()
        avg = a_buf[d]
        mom = 0.9 * v_buf[d] + avg
        v_buf[d] = mom
        m_buf[d] -= 0.7 * (avg + 0.9 * mom)
        back += started(
            [
                copy(m_buf.at[d], nm_ref.at[:, :, at[d]], sem.at[3, d]),
                copy(v_buf.at[d], nv_ref.at[:, :, at[d]], sem.at[4, d]),
            ]
        )
    for done in back:
        done.wait()


def along_yc(pieces):
    got = [pieces[0]] + [None] * (NYC - 1)
    for d in SHIFTS:
        got[d] = lax.ppermute(pieces[d], YC, [(i, ahead(i, d)) for i in range(NYC)])
    return got


def across(value):
    return lax.all_to_all(value, XZ, split_axis=0, concat_axis=0, tiled=True)


def shards(master, momentum, deltas, old_path, new_path, path_module, island_steps):
    modules = master.shape[0]
    me = lax.axis_index(YC).astype(jnp.int32).reshape(1)
    owner = (modules, 4, NYC, 2, *TILE)
    piece = (modules, 4, 2, *TILE)
    m = tiles(master).reshape(owner)
    v = tiles(momentum).reshape(owner)

    got = across(deltas[0].reshape(32, 64, 256))
    slots = (NYC, *piece)
    base = along_yc(call(base_kernel, [me, m, v], [piece] * NYC, 1, [slots] * 2, 3, WHOLE))
    base[0:1] = call(hold_kernel, base[0:1], [piece], 0, [], 1, 4 * MIB, (0,), (0,))
    isles = (8, 4, NYC, 2, *TILE)
    mixed = tiles(got).reshape(isles)
    [out] = call(
        pick_kernel,
        [me, old_path, new_path, path_module, island_steps, mixed, *base],
        [isles],
        5,
        [slots, slots, piece],
        2,
        20 * MIB,
        range(6, 6 + NYC),
    )
    avg = call(
        average_kernel,
        [me, old_path, path_module, island_steps, mixed],
        [piece] * NYC,
        4,
        [slots] * 2,
        2,
        61 * MIB,
    )
    out = jnp.swapaxes(out.reshape(32, NYC, 2, *TILE), 2, 3).reshape(32, 64, 256)
    landed = across(out)
    nm, nv = call(owner_kernel, [me, m, v, *along_yc(avg)], [owner] * 2, 1, [slots] * 3, 5, 61 * MIB)
    new_module = landed.reshape(deltas.shape)

    def whole(value):
        return jnp.swapaxes(value.reshape(modules, 64, *TILE), 1, 2).reshape(master.shape)

    return whole(nm), whole(nv), new_module


def solution(mesh):
    fine = Mesh(mesh.devices.reshape(4, 2, 4, 4, 2), ("x", "zh", "zl", "y", "c"))
    owners = P(None, ("x", "zh", "zl", "y", "c"), None)
    island = P(("x", "zh"), None, ("zl", "y", "c"))
    return jax.shard_map(
        shards,
        mesh=fine,
        in_specs=(owners, owners, island, P(), P(), P(), P()),
        out_specs=(owners, owners, island),
        check_vma=False,
    )
```

```python
import math

import jax
import jax.numpy as jnp
from jax import lax
from jax.experimental import pallas as pl
from jax.experimental.pallas import tpu as pltpu
from jax.sharding import Mesh
from jax.sharding import PartitionSpec as P

XZ = ("x", "zh", "zl")
YC = ("y", "c")
NY, NC = 4, 2
NYC = NY * NC
SHIFTS = (4, 5, 2, 6, 3, 7, 1)
TILE = (8, 128)
F32 = jnp.float32
MIB = 1 << 20
WHOLE = 64 * MIB - MIB // 4


def tiles(value):
    lead, rows, cols = value.shape[:-2], value.shape[-2], value.shape[-1]
    value = value.reshape(*lead, rows // 8, 8, cols // 128, 128)
    return jnp.swapaxes(value, -3, -2)


def call(body, ins, outs, scalars, scratch, sems, limit, near_in=(), near_out=()):
    smem, vmem, hbm = (pl.BlockSpec(memory_space=m) for m in (pltpu.SMEM, pltpu.VMEM, pltpu.HBM))
    moved = 4 * (sum(a.size for a in ins[scalars:]) + sum(math.prod(s) for s in outs))
    return pl.pallas_call(
        body,
        out_shape=[jax.ShapeDtypeStruct(s, F32) for s in outs],
        in_specs=[smem] * scalars + [vmem if i in near_in else hbm for i in range(scalars, len(ins))],
        out_specs=[vmem if i in near_out else hbm for i in range(len(outs))],
        scratch_shapes=[pltpu.VMEM(s, F32) for s in scratch] + [pltpu.SemaphoreType.DMA((sems, NYC))],
        cost_estimate=pl.CostEstimate(flops=moved, bytes_accessed=moved, transcendentals=0),
        compiler_params=pltpu.CompilerParams(vmem_limit_bytes=limit),
    )(*ins)


def started(copies):
    for copy in copies:
        copy.start()
    return copies


def ahead(me, d):
    return ((((me >> 1) + d // NC) & (NY - 1)) << 1) | ((me & 1) ^ (d % NC))


def behind(me, d):
    return ((((me >> 1) + NY - d // NC) & (NY - 1)) << 1) | ((me & 1) ^ (d % NC))


def base_kernel(me_ref, m_ref, v_ref, *refs):
    outs, (m_buf, v_buf, sem) = refs[:NYC], refs[NYC:]
    copy = pltpu.make_async_copy
    at = [ahead(me_ref[0], d) for d in range(NYC)]
    ms = [copy(m_ref.at[:, :, at[d]], m_buf.at[d], sem.at[0, d]) for d in range(NYC)]
    vs = [copy(v_ref.at[:, :, at[d]], v_buf.at[d], sem.at[1, d]) for d in range(NYC)]
    order = (*SHIFTS, 0)
    for d in order:
        started([ms[d], vs[d]])
    back = []
    for d in order:
        ms[d].wait()
        vs[d].wait()
        m_buf[d] -= (0.7 * 0.81) * v_buf[d]
        back += started([copy(m_buf.at[d], outs[d], sem.at[2, d])])
    for done in back:
        done.wait()


def lookup_kernel(me_ref, old_ref, new_ref, pm_ref, steps_ref, table, weights):
    islands = steps_ref.shape[0]
    table[0] = me_ref[0]
    old = [pm_ref[old_ref[j]] for j in range(islands)]
    for j in range(islands):
        total = jnp.int32(0)
        for i in range(islands):
            total += jnp.where(old[i] == old[j], steps_ref[i], 0)
        table[1 + j] = old[j]
        table[1 + islands + j] = pm_ref[new_ref[j]]
        splat = lambda s: jnp.full(TILE, s, jnp.int32).astype(F32)
        weights[j] = splat(steps_ref[j]) / splat(jnp.maximum(total, 1))


def lookup(*scalars):
    smem, vmem = (pl.BlockSpec(memory_space=m) for m in (pltpu.SMEM, pltpu.VMEM))
    islands = scalars[-1].shape[0]
    return pl.pallas_call(
        lookup_kernel,
        out_shape=[
            jax.ShapeDtypeStruct((1 + 2 * islands,), jnp.int32),
            jax.ShapeDtypeStruct((islands, *TILE), F32),
        ],
        in_specs=[smem] * len(scalars),
        out_specs=[smem, vmem],
        compiler_params=pltpu.CompilerParams(vmem_limit_bytes=4 * MIB),
    )(*scalars)


def add_up(avg, deltas, table, weights):
    avg[...] = jnp.zeros(avg.shape, F32)
    for j in range(weights.shape[0]):
        avg[table[1 + j]] += weights[j] * deltas[j]


def hold_kernel(src, out, sem):
    out[...] = src[...]


def pick_kernel(table, r_ref, weights, *refs):
    me, islands = table[0], weights.shape[0]
    bases, (out, r_buf, o_buf, avg, sem) = refs[:NYC], refs[NYC:]
    copy = pltpu.make_async_copy
    rows = [behind(me, d) for d in range(NYC)]
    rs = started([copy(r_ref.at[:, :, rows[d]], r_buf.at[d], sem.at[0, d]) for d in range(NYC)])
    back = []
    for d in range(NYC):
        rs[d].wait()
        add_up(avg, r_buf.at[d], table, weights)
        for j in range(islands):
            k = table[1 + islands + j]
            o_buf[d, j] = bases[d][k] - (0.7 * 1.9) * avg[k]
        back += started([copy(o_buf.at[d], out.at[:, :, rows[d]], sem.at[1, d])])
    for done in back:
        done.wait()


def average_kernel(table, r_ref, weights, *refs):
    averages, (r_buf, a_buf, sem) = refs[:NYC], refs[NYC:]
    copy = pltpu.make_async_copy
    rows = [ahead(table[0], d) for d in range(NYC)]
    order = (*SHIFTS, 0)
    rs = [copy(r_ref.at[:, :, rows[d]], r_buf.at[d], sem.at[0, d]) for d in range(NYC)]
    started([rs[d] for d in order])
    back = []
    for d in order:
        rs[d].wait()
        add_up(a_buf.at[d], r_buf.at[d], table, weights)
        back += started([copy(a_buf.at[d], averages[d], sem.at[1, d])])
    for done in back:
        done.wait()


def owner_kernel(me_ref, m_ref, v_ref, *refs):
    averages, (nm_ref, nv_ref), (m_buf, v_buf, a_buf, sem) = refs[:NYC], refs[NYC : NYC + 2], refs[NYC + 2 :]
    copy = pltpu.make_async_copy
    at = [behind(me_ref[0], d) for d in range(NYC)]
    ins = []
    for d in range(NYC):
        ins.append(
            started(
                [
                    copy(m_ref.at[:, :, at[d]], m_buf.at[d], sem.at[0, d]),
                    copy(v_ref.at[:, :, at[d]], v_buf.at[d], sem.at[1, d]),
                    copy(averages[d], a_buf.at[d], sem.at[2, d]),
                ]
            )
        )
    back = []
    for d in range(NYC):
        for done in ins[d]:
            done.wait()
        avg = a_buf[d]
        mom = 0.9 * v_buf[d] + avg
        v_buf[d] = mom
        m_buf[d] -= 0.7 * (avg + 0.9 * mom)
        back += started(
            [
                copy(m_buf.at[d], nm_ref.at[:, :, at[d]], sem.at[3, d]),
                copy(v_buf.at[d], nv_ref.at[:, :, at[d]], sem.at[4, d]),
            ]
        )
    for done in back:
        done.wait()


def along_yc(pieces):
    got = [pieces[0]] + [None] * (NYC - 1)
    for d in SHIFTS:
        got[d] = lax.ppermute(pieces[d], YC, [(i, ahead(i, d)) for i in range(NYC)])
    return got


def across(value):
    return lax.all_to_all(value, XZ, split_axis=0, concat_axis=0, tiled=True)


def shards(master, momentum, deltas, old_path, new_path, path_module, island_steps):
    modules = master.shape[0]
    me = lax.axis_index(YC).astype(jnp.int32).reshape(1)
    owner = (modules, 4, NYC, 2, *TILE)
    piece = (modules, 4, 2, *TILE)
    m = tiles(master).reshape(owner)
    v = tiles(momentum).reshape(owner)

    got = across(deltas[0].reshape(32, 64, 256))
    slots = (NYC, *piece)
    base = along_yc(call(base_kernel, [me, m, v], [piece] * NYC, 1, [slots] * 2, 3, WHOLE))
    base[0:1] = call(hold_kernel, base[0:1], [piece], 0, [], 1, 4 * MIB, (0,), (0,))
    table, weights = lookup(me, old_path, new_path, path_module, island_steps)
    isles = (8, 4, NYC, 2, *TILE)
    mixed = tiles(got).reshape(isles)
    [out] = call(
        pick_kernel,
        [table, mixed, weights, *base],
        [isles],
        1,
        [slots, slots, piece],
        2,
        20 * MIB,
        range(2, 3 + NYC),
    )
    avg = call(
        average_kernel,
        [table, mixed, weights],
        [piece] * NYC,
        1,
        [slots] * 2,
        2,
        61 * MIB,
        (2,),
    )
    out = jnp.swapaxes(out.reshape(32, NYC, 2, *TILE), 2, 3).reshape(32, 64, 256)
    landed = across(out)
    nm, nv = call(owner_kernel, [me, m, v, *along_yc(avg)], [owner] * 2, 1, [slots] * 3, 5, 61 * MIB)
    new_module = landed.reshape(deltas.shape)

    def whole(value):
        return jnp.swapaxes(value.reshape(modules, 64, *TILE), 1, 2).reshape(master.shape)

    return whole(nm), whole(nv), new_module


def solution(mesh):
    fine = Mesh(mesh.devices.reshape(4, 2, 4, 4, 2), ("x", "zh", "zl", "y", "c"))
    owners = P(None, ("x", "zh", "zl", "y", "c"), None)
    island = P(("x", "zh"), None, ("zl", "y", "c"))
    return jax.shard_map(
        shards,
        mesh=fine,
        in_specs=(owners, owners, island, P(), P(), P(), P()),
        out_specs=(owners, owners, island),
        check_vma=False,
    )
```
